32 devices in a mesh: fsdp: 4 (over z), context: 4 (over y, x), tensor: 2 (over core).
Axes of the slice: x: 2, y: 2, z: 4, core: 2. Of those that a mesh axis runs over, the one named last changes fastest.
Arguments:
- hidden: bfloat16 [16384, 1024], P(('fsdp', 'context')), may hold values from -6 to 6
- d_mixed: bfloat16 [16384, 1024], P(('fsdp', 'context')), may hold values from -6 to 6
- seq_lengths: int32 [4, 3], P('fsdp'), may hold values from 1 to 2048, 4096 in all within a row
- norm_gain: float32 [1024], replicated, may hold values from 0.5 to 1.5
- w_gate: bfloat16 [1024, 2048], P(('fsdp', 'context'), 'tensor'), may hold values from -0.1875 to 0.1875
- w_x: bfloat16 [1024, 2048], P(('fsdp', 'context'), 'tensor'), may hold values from -0.1875 to 0.1875
- w_bc: bfloat16 [1024, 256], P(('fsdp', 'context')), may hold values from -0.1875 to 0.1875
- w_dt: bfloat16 [1024, 32], P(('fsdp', 'context'), 'tensor'), may hold values from -0.09375 to 0.09375
- conv_x: float32 [4, 2048], P(None, 'tensor'), may hold values from -2 to 2
- conv_x_bias: float32 [2048], P('tensor'), may hold values from -1.5 to 1.5
- conv_bc: float32 [4, 256], replicated, may hold values from -2 to 2
- conv_bc_bias: float32 [256], replicated, may hold values from -1.5 to 1.5
- dt_bias: float32 [32], P('tensor'), may hold values from -8 to -2.5
- a_log: float32 [32], P('tensor'), may hold values from 0 to 2.77
- d_skip: float32 [32], P('tensor'), may hold values from 0.5 to 1.5
- gate_gain: float32 [2048], P('tensor'), may hold values from 0.5 to 1.5
- w_out: bfloat16 [2048, 1024], P('tensor', ('fsdp', 'context')), may hold values from -0.125 to 0.125
Outputs:
- mixed: bfloat16 [16384, 1024], P(('fsdp', 'context'), 'tensor')
- grad_hidden: float32 [16384, 1024], P(('fsdp', 'context'), 'tensor')
- grad_norm_gain: float32 [1024], P('tensor')
- grad_w_gate: float32 [1024, 2048], P(('fsdp', 'context'), 'tensor')
- grad_w_x: float32 [1024, 2048], P(('fsdp', 'context'), 'tensor')
- grad_w_bc: float32 [1024, 256], P(('fsdp', 'context'))
- grad_w_dt: float32 [1024, 32], P(('fsdp', 'context'), 'tensor')
- grad_conv_x: float32 [4, 2048], P(None, 'tensor')
- grad_conv_x_bias: float32 [2048], P('tensor')
- grad_conv_bc: float32 [4, 256], replicated
- grad_conv_bc_bias: float32 [256], replicated
- grad_dt_bias: float32 [32], P('tensor')
- grad_a_log: float32 [32], P('tensor')
- grad_d_skip: float32 [32], P('tensor')
- grad_gate_gain: float32 [2048], P('tensor')
- grad_w_out: float32 [2048, 1024], P('tensor', ('fsdp', 'context'))
The draws below stay inside these ranges and needn't reach their ends.
Inputs may be any that keep to these rules, and one draw needn't show every extreme that they name: `seq_lengths`: row f lists, in order, the lengths of the 3 sequences packed into token group f; they add up to 4096, and the longest is exactly 2048.
All inputs are finite; a program needn't handle non-finite values.
Results may differ from the reference program's by a relative error of at most 0.02.
Values may be sent and summed in bfloat16 or wider, within the bound.
A program may use at most 320 MiB of HBM per device.

```python
import math
import jax
import jax.numpy as jnp
import numpy as np
from jax import lax

D = 1024
HEADS = 32
HEADDIM = 64
STATE = 128
INNER = 2048
CONV = 4
SPAN = 256
SEQS = 3
GROUP_TOK = 4096
MAX_LEN = 2048
TOKENS = 16384
N_FSDP = 4
N_TENSOR = 2


def draw_dt_bias(key, part):
    values = jax.random.uniform(key, (HEADS,), jnp.float32, -7.0, -2.5)
    return values


def levels(stream_key, shape, split, low, top_value):
    gain = 1.0
    for position, blocks in split:
        draws = jax.random.uniform(jax.random.fold_in(jax.random.fold_in(stream_key, 6), position), (blocks,), jnp.float32, low / len(split), top_value / len(split))
        gain = gain * jnp.repeat(jnp.exp(draws), shape[position] // blocks).reshape((-1,) + (1,) * (len(shape) - 1 - position))
    return gain


def split_up(count, total, reach, lean):
    loads = [(1 << 20) // math.isqrt(standing ** lean) + 1 for standing in range(2, count + 1)]
    rest, given = total - reach - (count - 1), [1] * (count - 1)
    while rest > 0:
        free = [i for i in range(count - 1) if given[i] < reach]
        pool, budget = sum([loads[i] for i in free]), rest
        for i in free:
            addition = min(reach - given[i], max(1, budget * loads[i] // pool), rest)
            given[i] = given[i] + addition
            rest = rest - addition
    return np.array([reach] + given)


def uneven(stream_key, count, total, most, lean):
    if count == 2:
        one = jax.random.randint(stream_key, (), max(1, total - most), min(most, total - 1) + 1)
        return jnp.stack([one, total - one])
    sizes = jnp.asarray(split_up(count, total, most, lean), jnp.int32)
    twos = (count - 1) // 2
    donor, sink = sizes[1:1 + 2 * twos:2], sizes[2:2 + 2 * twos:2]
    margin = jnp.minimum(donor - 1, most - sink)
    shifted = jax.random.randint(jax.random.fold_in(stream_key, 1), (twos,), 0, 1 << 20) % (margin + 1)
    sizes = sizes.at[1:1 + 2 * twos:2].set(donor - shifted).at[2:2 + 2 * twos:2].set(sink + shifted)
    return sizes[jax.random.permutation(jax.random.fold_in(stream_key, 2), count)]


def centred(own_key, dims, deviation, most, pieces=(), held_as=jnp.bfloat16):
    array = jax.random.normal(own_key, dims, jnp.float32) * deviation
    if len(pieces) > 0:
        array = levels(own_key, dims, pieces, -0.22, 0.18) * array
    return jnp.clip(array, min=-most, max=most).astype(held_as)


def setup_inputs(seed: int = 0) -> dict:
    splits = jax.random.split(jax.random.key(seed), 18)
    hidden = centred(splits[0], (TOKENS, D), 1.0, 6.0, ((0, 16),))
    d_mixed = centred(splits[1], (TOKENS, D), 1.0, 6.0, ((0, 16),))
    seq_lengths = jax.vmap(lambda own: uneven(own, SEQS, GROUP_TOK, MAX_LEN, 2))(jax.random.split(splits[2], N_FSDP)).reshape((N_FSDP, SEQS)).astype(jnp.int32)
    norm_gain = jnp.clip(1.0 + 0.1 * jax.random.normal(splits[3], (D,), jnp.float32), 0.5, 1.5)
    w_gate = centred(splits[4], (D, INNER), D ** -0.5, 0.1875, ((0, 16), (1, 2)))
    w_x = centred(splits[5], (D, INNER), D ** -0.5, 0.1875, ((0, 16), (1, 2)))
    w_bc = centred(splits[6], (D, 2 * STATE), D ** -0.5, 0.1875, ((0, 16),))
    w_dt = centred(splits[7], (D, HEADS), (4 * D) ** -0.5, 0.09375, ((0, 16), (1, 2)))
    conv_x = centred(splits[8], (CONV, INNER), 0.4, 2.0, ((1, 2),), jnp.float32)
    conv_x_bias = centred(splits[9], (INNER,), 0.3, 1.5, ((0, 2),), jnp.float32)
    conv_bc = centred(splits[10], (CONV, 2 * STATE), 0.4, 2.0, (), jnp.float32)
    conv_bc_bias = centred(splits[11], (2 * STATE,), 0.3, 1.5, (), jnp.float32)
    dt_bias = draw_dt_bias(jax.random.fold_in(splits[17], 71), 0)
    a_log = jnp.clip(2.77 * jax.random.uniform(splits[13], (HEADS,), jnp.float32) ** levels(splits[13], (HEADS,), ((0, 2),), -0.2, 0.2), 0.0, 2.77)
    d_skip = jnp.clip(0.5 + 1.0 * jax.random.uniform(splits[14], (HEADS,), jnp.float32) ** levels(splits[14], (HEADS,), ((0, 2),), -0.2, 0.2), 0.5, 1.5)
    gate_gain = jnp.clip(1.0 + 0.1 * jax.random.normal(splits[15], (INNER,), jnp.float32), 0.5, 1.5)
    w_out = centred(splits[16], (INNER, D), INNER ** -0.5, 0.125, ((0, 2), (1, 16)))
    return dict(hidden=hidden, d_mixed=d_mixed, seq_lengths=seq_lengths, norm_gain=norm_gain, w_gate=w_gate, w_x=w_x, w_bc=w_bc, w_dt=w_dt, conv_x=conv_x, conv_x_bias=conv_x_bias, conv_bc=conv_bc, conv_bc_bias=conv_bc_bias, dt_bias=dt_bias, a_log=a_log, d_skip=d_skip, gate_gain=gate_gain, w_out=w_out)


EPSILON = 1e-05
PRECISE = lax.Precision.HIGHEST

def segment_ids(lengths, positions):
    starts = jnp.cumsum(lengths).astype(jnp.int32) - lengths
    inside = (positions[:, None] >= starts[None, 1:]).astype(jnp.int32)
    counted = lax.optimization_barrier(jnp.sum(inside, axis=1)).astype(jnp.int32)
    return jnp.where(positions < 0, -1, counted).astype(jnp.int32)

def causal_conv(values, edge_values, weight, conv_shift, segment, edge_segment):
    tap_count = weight.shape[0]
    length = values.shape[0]
    joined = jnp.concatenate([edge_values, values], axis=0)
    joined_segment = jnp.concatenate([edge_segment, segment], axis=0)
    summed = jnp.zeros_like(values) + conv_shift[None, :]
    for offset in range(tap_count):
        matched = joined_segment[offset:offset + length] == segment
        summed = summed + jnp.where(matched[:, None], joined[offset:offset + length], 0.0) * weight[offset][None, :]
    return jax.nn.silu(summed)

def span_scan(x_heads, delta, decay_rate, b_rows, c_rows, segment, seg_before, state):
    length, head_count, head_size = x_heads.shape
    blocks = length // SPAN
    span_last = segment[SPAN - 1::SPAN]
    prev_segment = jnp.concatenate([seg_before[None], span_last[:-1]])
    stacked = (x_heads.reshape(blocks, SPAN, head_count, head_size), delta.reshape(blocks, SPAN, head_count), b_rows.reshape(blocks, SPAN, -1), c_rows.reshape(blocks, SPAN, -1), segment.reshape(blocks, SPAN), prev_segment)

    def advance(carried, block):
        x_block, dt_block, b_block, c_block, seg_block, seg_prev = block
        rates = (dt_block * decay_rate[None, :]).T
        cumulative = jnp.cumsum(rates, axis=1)
        indices = jnp.arange(SPAN)
        causal = (indices[:, None] >= indices[None, :]) & (seg_block[:, None] == seg_block[None, :])
        spread = jnp.where(causal[None], cumulative[:, :, None] - cumulative[:, None, :], 0.0)
        decay = jnp.where(causal[None], jnp.exp(spread), 0.0)
        scores = jnp.dot(c_block, b_block.T, precision=PRECISE)
        mixing = decay * scores[None] * dt_block.T[:, None, :]
        within = jnp.einsum('hts,shp->thp', mixing, x_block, precision=PRECISE)
        leading = jnp.where((seg_block == seg_prev)[None, :], jnp.exp(cumulative), 0.0)
        from_state = jnp.einsum('tn,hpn->thp', c_block, carried, precision=PRECISE) * leading.T[:, :, None]
        trailing = jnp.where((seg_block == seg_block[-1])[None, :], jnp.exp(cumulative[:, -1:] - cumulative), 0.0) * dt_block.T
        weighted = x_block * trailing.T[:, :, None]
        added = jnp.einsum('shp,sn->hpn', weighted, b_block, precision=PRECISE)
        renewed = leading[:, -1][:, None, None] * carried + added
        return (renewed, within + from_state)
    final_state, outputs = lax.scan(advance, state, stacked)
    return (outputs.reshape(length, head_count, head_size), final_state)

def mixer_core(x_act, bc_act, dt_input, z_input, dt_bias, a_log, d_skip, state, segment, seg_before):
    length = x_act.shape[0]
    head_count = dt_input.shape[1]
    x_heads = x_act.reshape(length, head_count, -1)
    delta = jax.nn.softplus(dt_input + dt_bias[None, :])
    decay_rate = -jnp.exp(a_log)
    state_width = bc_act.shape[1] // 2
    output, unused = span_scan(x_heads, delta, decay_rate, bc_act[:, :state_width], bc_act[:, state_width:], segment, seg_before, state)
    output = output + d_skip[None, :, None] * x_heads
    return output.reshape(length, -1) * jax.nn.silu(z_input)

def reference(hidden, d_mixed, seq_lengths, norm_gain, w_gate, w_x, w_bc, w_dt, conv_x, conv_x_bias, conv_bc, conv_bc_bias, dt_bias, a_log, d_skip, gate_gain, w_out):
    model_width = w_gate.shape[0]
    inner_width = w_gate.shape[1]
    head_count = w_dt.shape[1]
    group_tokens = GROUP_TOK
    hidden_groups = hidden.reshape(N_FSDP, group_tokens, model_width)
    dmix_groups = d_mixed.reshape(N_FSDP, group_tokens, model_width)
    conv_weight = jnp.concatenate([conv_x, conv_bc], axis=1)
    conv_shift = jnp.concatenate([conv_x_bias, conv_bc_bias])
    edge_values = jnp.zeros((CONV - 1, conv_weight.shape[1]), jnp.float32)
    positions = jnp.arange(group_tokens, dtype=jnp.int32)
    edge_positions = jnp.arange(CONV - 1, dtype=jnp.int32) - (CONV - 1)
    zero_state = jnp.zeros((head_count, HEADDIM, STATE), jnp.float32)
    seg_start = jnp.full((), -1, jnp.int32)

    def group_pass(sums, inputs):
        hidden_rows, dmix_rows, lengths = inputs
        segment = segment_ids(lengths, positions)
        edge_segment = segment_ids(lengths, edge_positions)
        widened = hidden_rows.astype(jnp.float32)
        row_scale = lax.rsqrt(lax.optimization_barrier(jnp.mean(widened * widened, axis=1, keepdims=True)) + EPSILON)
        normed = (widened * row_scale * norm_gain[None, :]).astype(jnp.bfloat16)
        z_proj = lax.optimization_barrier(jnp.dot(normed, w_gate, preferred_element_type=jnp.float32).astype(jnp.bfloat16))
        x_proj = jnp.dot(normed, w_x, preferred_element_type=jnp.float32).astype(jnp.bfloat16)
        bc_proj = jnp.dot(normed, w_bc, preferred_element_type=jnp.float32).astype(jnp.bfloat16)
        dt_proj = lax.optimization_barrier(jnp.dot(normed, w_dt, preferred_element_type=jnp.float32).astype(jnp.bfloat16))
        conv_input = lax.optimization_barrier(jnp.concatenate([x_proj, bc_proj], axis=1))

        def conv_piece(values, weight, shift_row):
            return causal_conv(values, edge_values, weight, shift_row, segment, edge_segment)
        activated, conv_back = jax.vjp(conv_piece, conv_input.astype(jnp.float32), conv_weight, conv_shift)
        act_rounded = lax.optimization_barrier(activated.astype(jnp.bfloat16))
        x_act = act_rounded[:, :inner_width].astype(jnp.float32)
        bc_act = act_rounded[:, inner_width:].astype(jnp.float32)
        z_input = z_proj.astype(jnp.float32)
        dt_input = dt_proj.astype(jnp.float32)

        def core(x_in, bc_in, dt_in, z_in, bias_in, alog_in, skip_in):
            return mixer_core(x_in, bc_in, dt_in, z_in, bias_in, alog_in, skip_in, zero_state, segment, seg_start)
        gated, core_back = jax.vjp(core, x_act, bc_act, dt_input, z_input, dt_bias, a_log, d_skip)
        gate_scale = lax.rsqrt(lax.optimization_barrier(jnp.mean(gated * gated, axis=1, keepdims=True)) + EPSILON)
        normed_out = (gated * gate_scale * gate_gain[None, :]).astype(jnp.bfloat16)
        partials = jnp.einsum('tgc,gcd->gtd', normed_out.reshape(group_tokens, N_TENSOR, -1).astype(jnp.float32), w_out.reshape(N_TENSOR, -1, model_width).astype(jnp.float32))
        partials = lax.optimization_barrier(partials.astype(jnp.bfloat16))
        mixed_rows = (widened + lax.optimization_barrier(jnp.sum(partials.astype(jnp.float32), axis=0))).astype(jnp.bfloat16)
        grad_norm_out = jnp.dot(dmix_rows, w_out.T, preferred_element_type=jnp.float32)
        out_term = jnp.dot(normed_out.T, dmix_rows, preferred_element_type=jnp.float32)
        gain_term = lax.optimization_barrier(jnp.sum(grad_norm_out * gated * gate_scale, axis=0))
        scaled_grad = grad_norm_out * gate_gain[None, :]
        grad_gated = gate_scale * scaled_grad - gated * gate_scale ** 3 * lax.optimization_barrier(jnp.mean(scaled_grad * gated, axis=1, keepdims=True))
        grad_xact, grad_bcact, grad_dtin, grad_zin, grad_dtbias, grad_alog, grad_dskip = core_back(grad_gated)
        grad_conv_in, grad_convw, grad_convb = conv_back(jnp.concatenate([grad_xact, grad_bcact], axis=1))
        grad_zb = grad_zin.astype(jnp.bfloat16)
        grad_xb = grad_conv_in[:, :inner_width].astype(jnp.bfloat16)
        grad_bcb = grad_conv_in[:, inner_width:].astype(jnp.bfloat16)
        grad_dtb = grad_dtin.astype(jnp.bfloat16)
        gate_term = jnp.dot(normed.T, grad_zb, preferred_element_type=jnp.float32)
        xin_term = jnp.dot(normed.T, grad_xb, preferred_element_type=jnp.float32)
        bc_term = jnp.dot(normed.T, grad_bcb, preferred_element_type=jnp.float32)
        dt_term = jnp.dot(normed.T, grad_dtb, preferred_element_type=jnp.float32)

        def block_terms(grad_rows, weight):
            return jnp.einsum('tgc,dgc->gtd', grad_rows.reshape(group_tokens, N_TENSOR, -1).astype(jnp.float32), weight.reshape(model_width, N_TENSOR, -1).astype(jnp.float32))
        head_parts = block_terms(grad_zb, w_gate) + block_terms(grad_xb, w_x) + block_terms(grad_dtb, w_dt)
        head_parts = head_parts + block_terms(grad_bcb, w_bc)
        head_parts = lax.optimization_barrier(head_parts.astype(jnp.bfloat16))
        grad_normed = lax.optimization_barrier(jnp.sum(head_parts.astype(jnp.float32), axis=0))
        norm_term = lax.optimization_barrier(jnp.sum(grad_normed * widened * row_scale, axis=0))
        gained = grad_normed * norm_gain[None, :]
        grad_rows = dmix_rows.astype(jnp.float32) + row_scale * gained - widened * row_scale ** 3 * lax.optimization_barrier(jnp.mean(gained * widened, axis=1, keepdims=True))
        terms = (norm_term, gate_term, xin_term, bc_term, dt_term, grad_convw[:, :inner_width], grad_convb[:inner_width], grad_convw[:, inner_width:], grad_convb[inner_width:], grad_dtbias, grad_alog, grad_dskip, gain_term, out_term)
        renewed = tuple((older + newer for older, newer in zip(sums, terms)))
        return (renewed, (mixed_rows, grad_rows))
    start_sums = (jnp.zeros_like(norm_gain), jnp.zeros(w_gate.shape, jnp.float32), jnp.zeros(w_x.shape, jnp.float32), jnp.zeros(w_bc.shape, jnp.float32), jnp.zeros(w_dt.shape, jnp.float32), jnp.zeros_like(conv_x), jnp.zeros_like(conv_x_bias), jnp.zeros_like(conv_bc), jnp.zeros_like(conv_bc_bias), jnp.zeros_like(dt_bias), jnp.zeros_like(a_log), jnp.zeros_like(d_skip), jnp.zeros_like(gate_gain), jnp.zeros(w_out.shape, jnp.float32))
    sums, outputs = lax.scan(group_pass, start_sums, (hidden_groups, dmix_groups, seq_lengths))
    mixed = outputs[0].reshape(-1, model_width)
    grad_hidden = outputs[1].reshape(-1, model_width)
    return (mixed, grad_hidden, sums[0], sums[1], sums[2], sums[3], sums[4], sums[5], sums[6], sums[7], sums[8], sums[9], sums[10], sums[11], sums[12], sums[13])
```

```python
import functools
import jax
import jax.numpy as jnp
from jax import lax
from jax.experimental import pallas as pl
from jax.experimental.pallas import tpu as pltpu
from jax.sharding import PartitionSpec as P

EPSILON = 1e-05
HIGH = lax.Precision.HIGHEST
BF = jnp.bfloat16
F32 = jnp.float32
CHUNK = 128
NEG = -1e30
NT = (((1,), (1,)), ((), ()))
TN = (((0,), (0,)), ((), ()))


def dot(a, b, dims=(((1,), (0,)), ((), ())), precision=None):
    return lax.dot_general(a, b, dims, precision=precision, preferred_element_type=F32)


def split2(value):
    high = value.astype(BF)
    return high, (value - high.astype(F32)).astype(BF)


def expand(value, spread):
    high, low = split2(value)
    return dot(high, spread) + dot(low, spread)


def per_head(value, spread):
    high, low = split2(value)
    return dot(high, spread, NT) + dot(low, spread, NT)


def seg_at(info_ref, count, positions):
    found = jnp.where(positions < 0, -1, 0)
    for k in range(1, count):
        found = found + jnp.where(positions >= info_ref[k], 1, 0)
    return found


def softplus(v):
    return jnp.maximum(v, 0.0) + jnp.log1p(jnp.exp(-jnp.abs(v)))


def chunk_terms(info_ref, count, chunk, size, dt_ref, bias_ref, alog_ref, spread):
    first = info_ref[0] + chunk * size
    rows = lax.broadcasted_iota(jnp.int32, (size, size), 0)
    cols = lax.broadcasted_iota(jnp.int32, (size, size), 1)
    seg_row = seg_at(info_ref, count, first + rows)
    seg_col = seg_at(info_ref, count, first + cols)
    seg_one = seg_at(info_ref, count, first + lax.broadcasted_iota(jnp.int32, (size, 1), 0))
    seg_prev = seg_at(info_ref, count, first - 1)
    seg_last = seg_at(info_ref, count, first + size - 1)
    raw = dt_ref[...].astype(F32) + bias_ref[...]
    delta = softplus(raw)
    decay_rate = -jnp.exp(alog_ref[...])
    rates = delta * decay_rate
    lower = jnp.where(rows >= cols, 1.0, 0.0)
    cum = dot(lower, rates, precision=HIGH)
    upper = jnp.where(rows <= cols, 1.0, 0.0)
    cum_t = dot(rates, upper, TN, precision=HIGH)
    lead = jnp.where(seg_one == seg_prev, jnp.exp(cum), 0.0)
    trail = jnp.where(seg_one == seg_last, jnp.exp(cum[size - 1 :, :] - cum), 0.0)
    same = seg_row == seg_col
    return (rows, cols, same, seg_one, raw, delta, decay_rate, cum, cum_t, lead, trail, upper)


def pair_width(heads, width):
    head = width // heads
    per = max(1, 128 // head)
    while heads % per:
        per -= 1
    return head, per


def forward_kernel(
    count, heads, info_ref, x_ref, bc_ref, dt_ref, bias_ref, alog_ref, spread_ref,
    y_ref, full_ref, state_ref, final_ref, carry, total,
):
    size, width = x_ref.shape
    states = bc_ref.shape[1] // 2
    chunk = pl.program_id(0)

    @pl.when(chunk == 0)
    def _():
        carry[...] = jnp.zeros_like(carry)
        total[...] = jnp.zeros_like(total)

    spread = spread_ref[...]
    (rows, cols, same, seg_one, raw, delta, decay_rate, cum, cum_t, lead, trail, upper) = (
        chunk_terms(info_ref, count, chunk, size, dt_ref, bias_ref, alog_ref, spread)
    )
    neg = jnp.where((rows >= cols) & same, 0.0, NEG)
    seg_before = seg_at(info_ref, count, info_ref[0] - 1)
    full_ref[...] = jnp.where(seg_one == seg_before, jnp.exp(cum + total[0:1, :]), 0.0)
    total[0:1, :] = total[0:1, :] + cum[size - 1 :, :]
    x = x_ref[...].astype(F32)
    xdt = (x * expand(delta, spread)).astype(BF)
    b_rows = bc_ref[:, :states]
    c_rows = bc_ref[:, states:]
    scores = dot(c_rows, b_rows, NT)
    held = carry[...]
    held_b = held.astype(BF)
    state_ref[0] = held_b
    lead_wide = expand(lead, spread)
    y_ref[...] = dot(c_rows, held_b) * lead_wide
    head, per = pair_width(heads, width)
    span = head * per
    lane = lax.broadcasted_iota(jnp.int32, (size, span), 1) // head
    for group in range(heads // per):
        at = slice(group * span, (group + 1) * span)
        xg = xdt[:, at]
        out = None
        for k in range(per):
            h = group * per + k
            decay = jnp.exp(cum[:, h : h + 1] - cum_t[h : h + 1, :] + neg)
            part = dot((decay * scores).astype(BF), xg)
            out = part if out is None else jnp.where(lane >= k, part, out)
        y_ref[:, at] = y_ref[:, at] + out
    weighted = (xdt.astype(F32) * expand(trail, spread)).astype(BF)
    carry[...] = lead_wide[size - 1 :, :] * held + dot(b_rows, weighted, TN)

    @pl.when(chunk == pl.num_programs(0) - 1)
    def _():
        final_ref[:states, :] = carry[...]
        final_ref[states:, :] = expand(
            jnp.broadcast_to(full_ref[size - 1 :, :], (8, heads)), spread
        )


def backward_kernel(
    count, heads, info_ref, x_ref, bc_ref, dt_ref, bias_ref, alog_ref, skip_ref, spread_ref,
    y_ref, dy_ref, state_ref, start_ref, in_ref, leave_ref,
    dx_ref, dbc_ref, ddt_ref, sums_ref, carry,
):
    size, width = x_ref.shape
    states = bc_ref.shape[1] // 2
    step = pl.program_id(0)
    chunk = pl.num_programs(0) - 1 - step

    @pl.when(step == 0)
    def _():
        carry[...] = leave_ref[...]
        sums_ref[...] = jnp.zeros_like(sums_ref)

    spread = spread_ref[...]
    (rows, cols, same, seg_one, raw, delta, decay_rate, cum, cum_t, lead, trail, upper) = (
        chunk_terms(info_ref, count, chunk, size, dt_ref, bias_ref, alog_ref, spread)
    )
    neg = jnp.where((rows <= cols) & same, 0.0, NEG)
    x = x_ref[...].astype(F32)
    delta_wide = expand(delta, spread)
    xdt = (x * delta_wide).astype(BF)
    xdt_f = xdt.astype(F32)
    dy = dy_ref[...]
    dy_f = dy.astype(F32)
    b_rows = bc_ref[:, :states]
    c_rows = bc_ref[:, states:]
    scores = dot(b_rows, c_rows, NT)
    grad_state = carry[...]
    grad_state_b = grad_state.astype(BF)
    held = state_ref[0].astype(F32) + expand(start_ref[0], spread)[0:1, :] * in_ref[...]
    held_b = held.astype(BF)
    trail_wide = expand(trail, spread)
    lead_wide = expand(lead, spread)
    state_part = dot(b_rows, grad_state_b) * trail_wide
    dx_ref[...] = state_part
    head, per = pair_width(heads, width)
    span = head * per
    lane = lax.broadcasted_iota(jnp.int32, (size, span), 1) // head
    dscore = jnp.zeros((size, size), F32)
    for group in range(heads // per):
        at = slice(group * span, (group + 1) * span)
        xg = xdt[:, at]
        dyg = dy[:, at]
        out = None
        for k in range(per):
            h = group * per + k
            decay = jnp.exp(cum_t[h : h + 1, :] - cum[:, h : h + 1] + neg)
            part = dot((decay * scores).astype(BF), dyg)
            out = part if out is None else jnp.where(lane >= k, part, out)
            own = jnp.where(lane == k, xg, jnp.zeros_like(xg))
            dscore = dscore + decay * dot(own, dyg, NT)
        dx_ref[:, at] = dx_ref[:, at] + out
    dxdt = dx_ref[...]
    dscore_b = dscore.astype(BF)
    led = (dy_f * lead_wide).astype(BF)
    weighted = (xdt_f * trail_wide).astype(BF)
    dbc_ref[:, :states] = dot(dscore_b, c_rows) + dot(weighted, grad_state_b, NT)
    dbc_ref[:, states:] = dot(dscore_b, b_rows, TN) + dot(led, held_b, NT)
    flows = per_head(dy_f * y_ref[...] - xdt_f * dxdt, spread)
    kept = jnp.sum(xdt_f * state_part, axis=0, keepdims=True) + lead_wide[
        size - 1 :, :
    ] * jnp.sum(held * grad_state, axis=0, keepdims=True)
    at_end = per_head(jnp.broadcast_to(kept, (8, width)), spread)[0:1, :]
    drate = dot(upper, flows, precision=HIGH) + at_end
    ddelta = per_head(x * dxdt, spread) + drate * decay_rate
    draw = ddelta * jax.nn.sigmoid(raw)
    ddt_ref[...] = draw
    skip_sum = per_head(
        jnp.broadcast_to(jnp.sum(dy_f * x, axis=0, keepdims=True), (8, width)), spread
    )[0:1, :]
    sums_ref[0:1, :] += jnp.sum(draw, axis=0, keepdims=True)
    sums_ref[1:2, :] += jnp.sum(drate * delta, axis=0, keepdims=True) * decay_rate
    sums_ref[2:3, :] += skip_sum
    skip_wide = expand(jnp.broadcast_to(skip_ref[...], (8, heads)), spread)[0:1, :]
    dx_ref[...] = dxdt * delta_wide + skip_wide * dy_f
    carry[...] = lead_wide[size - 1 :, :] * grad_state + dot(c_rows, led, TN)


def conv_back_kernel(
    count, taps, info_ref, v_ref, edge_ref, g_ref, w_ref, b_ref,
    out_ref, tail_ref, before_ref, grads_ref, ext, shifted_g,
):
    length, width = v_ref.shape
    first = info_ref[0]
    local = lax.broadcasted_iota(jnp.int32, (length, width), 0)
    ext[0:8, :] = edge_ref[...].astype(F32)
    ext[8 : 8 + length, :] = v_ref[...].astype(F32)
    pre = jnp.zeros((length, width), F32) + b_ref[...]
    own = seg_at(info_ref, count, first + local)
    for k in range(taps):
        moved = ext[8 - k : 8 - k + length, :]
        if k:
            moved = jnp.where(seg_at(info_ref, count, first + local - k) == own, moved, 0.0)
        pre = pre + moved * w_ref[taps - 1 - k : taps - k, :]
    sig = jax.nn.sigmoid(pre)
    grad = g_ref[...].astype(F32) * sig * (1.0 + pre * (1.0 - sig))
    grads_ref[...] = jnp.zeros_like(grads_ref)
    grads_ref[taps : taps + 1, :] = jnp.sum(grad, axis=0, keepdims=True)
    back = jnp.zeros((length, width), F32)
    early = jnp.zeros((8, width), F32)
    shifted_g[0:8, :] = jnp.zeros((8, width), F32)
    shifted_g[8 + length :, :] = jnp.zeros((8, width), F32)
    for k in range(taps):
        kept = grad
        if k:
            kept = jnp.where(seg_at(info_ref, count, first + local - k) == own, grad, 0.0)
        moved = ext[8 - k : 8 - k + length, :]
        at = taps - 1 - k
        grads_ref[at : at + 1, :] = jnp.sum(kept * moved, axis=0, keepdims=True)
        shifted_g[8 : 8 + length, :] = kept
        weight = w_ref[at : at + 1, :]
        back = back + shifted_g[8 + k : 8 + k + length, :] * weight
        early = early + shifted_g[k : k + 8, :] * weight
    out_ref[...] = back.astype(BF)
    tail_ref[...] = back[length - 8 :, :]
    before_ref[...] = early


def whole(shape):
    return pl.BlockSpec(shape, lambda i: (0,) * len(shape))


SMEM = pl.BlockSpec(memory_space=pltpu.SMEM)


def conv_back(info, count, values, edge, grad, weight, shift):
    length, width = values.shape
    taps = weight.shape[0]
    block = 128
    col = lambda r: pl.BlockSpec((r, block), lambda i: (0, i))
    return pl.pallas_call(
        functools.partial(conv_back_kernel, count, taps),
        grid=(width // block,),
        in_specs=[SMEM, col(length), col(8), col(length), col(taps), col(1)],
        out_specs=[col(length), col(8), col(8), col(8)],
        out_shape=[
            jax.ShapeDtypeStruct((length, width), BF),
            jax.ShapeDtypeStruct((8, width), F32),
            jax.ShapeDtypeStruct((8, width), F32),
            jax.ShapeDtypeStruct((8, width), F32),
        ],
        scratch_shapes=[pltpu.VMEM((length + 8, block), F32), pltpu.VMEM((length + 16, block), F32)],
        name="conv_back",
    )(info, values, edge, grad, weight, shift)


def scan_forward(info, count, x, bc, dt, bias, alog, spread):
    length, width = x.shape
    heads = dt.shape[1]
    states = bc.shape[1] // 2
    chunks = length // CHUNK
    row = lambda c: pl.BlockSpec((CHUNK, c), lambda i: (i, 0))
    return pl.pallas_call(
        functools.partial(forward_kernel, count, heads),
        grid=(chunks,),
        in_specs=[
            SMEM, row(width), row(2 * states), row(heads),
            whole((1, heads)), whole((1, heads)), whole((heads, width)),
        ],
        out_specs=[
            row(width), row(heads),
            pl.BlockSpec((1, states, width), lambda i: (i, 0, 0)), whole((states + 8, width)),
        ],
        out_shape=[
            jax.ShapeDtypeStruct((length, width), F32),
            jax.ShapeDtypeStruct((length, heads), F32),
            jax.ShapeDtypeStruct((chunks, states, width), BF),
            jax.ShapeDtypeStruct((states + 8, width), F32),
        ],
        scratch_shapes=[pltpu.VMEM((states, width), F32), pltpu.VMEM((8, heads), F32)],
        name="scan_forward",
    )(info, x, bc, dt, bias, alog, spread)


def scan_backward(info, count, x, bc, dt, bias, alog, skip, spread, y, dy, states_at, start, state_in, leaving):
    length, width = x.shape
    heads = dt.shape[1]
    states = bc.shape[1] // 2
    chunks = length // CHUNK
    row = lambda c: pl.BlockSpec((CHUNK, c), lambda i: (chunks - 1 - i, 0))
    return pl.pallas_call(
        functools.partial(backward_kernel, count, heads),
        grid=(chunks,),
        in_specs=[
            SMEM, row(width), row(2 * states), row(heads),
            whole((1, heads)), whole((1, heads)), whole((1, heads)), whole((heads, width)),
            row(width), row(width),
            pl.BlockSpec((1, states, width), lambda i: (chunks - 1 - i, 0, 0)),
            pl.BlockSpec((1, 8, heads), lambda i: (chunks - 1 - i, 0, 0)),
            whole((states, width)), whole((states, width)),
        ],
        out_specs=[row(width), row(2 * states), row(heads), whole((8, heads))],
        out_shape=[
            jax.ShapeDtypeStruct((length, width), F32),
            jax.ShapeDtypeStruct((length, 2 * states), F32),
            jax.ShapeDtypeStruct((length, heads), F32),
            jax.ShapeDtypeStruct((8, heads), F32),
        ],
        scratch_shapes=[pltpu.VMEM((states, width), F32)],
        name="scan_backward",
    )(info, x, bc, dt, bias, alog, skip, spread, y, dy, states_at, start, state_in, leaving)


def ring(axis, step):
    count = lax.axis_size(axis)
    return [(source, (source + step) % count) for source in range(count)]


def shifted(value, axis, steps):
    count = lax.axis_size(axis)
    initial, last = (max(0, -steps), min(count, count - steps))
    return lax.ppermute(value, axis, [(source, source + steps) for source in range(initial, last)])


def total_over(value, axis):
    if lax.axis_size(axis) == 2:
        return value.astype(F32) + lax.ppermute(value, axis, ring(axis, 1)).astype(F32)
    return jnp.sum(gather_axis(value, axis, 0).astype(F32), axis=0)


def share_over(value, axis, dim):
    count, index = (lax.axis_size(axis), lax.axis_index(axis))
    size = value.shape[dim] // count
    part = lambda at: lax.dynamic_slice_in_dim(value, at * size, size, dim)
    result = part(index).astype(F32)
    for step in range(1, count):
        sent = part((index + step) % count)
        result = result + lax.ppermute(sent, axis, ring(axis, step)).astype(F32)
    return result


def gather_axis(value, axis, dim):
    count, index = (lax.axis_size(axis), lax.axis_index(axis))
    shape = value.shape[:dim] + (count,) + value.shape[dim:]
    result = lax.dynamic_update_index_in_dim(jnp.zeros(shape, value.dtype), value, index, dim)
    for step in range(1, count):
        got = lax.ppermute(value, axis, ring(axis, step))
        result = lax.dynamic_update_index_in_dim(result, got, (index - step) % count, dim)
    return result


def gather_rows(value):
    first = gather_axis(value, "fsdp", 0)
    second = gather_axis(first, "context", 1)
    return second.reshape(-1, value.shape[-1])


def scatter_axis(value, axis, dim):
    count, index = (lax.axis_size(axis), lax.axis_index(axis))
    part = lambda at: lax.dynamic_index_in_dim(value, at, dim, False)
    result = part(index).astype(F32)
    for step in range(1, count):
        sent = part((index + step) % count)
        result = result + lax.ppermute(sent, axis, ring(axis, step)).astype(F32)
    return result


def scatter_rows(value):
    fsdp, context = (lax.axis_size("fsdp"), lax.axis_size("context"))
    shaped = value.astype(BF).reshape(fsdp, context, -1, value.shape[-1])
    return scatter_axis(scatter_axis(shaped, "context", 1).astype(BF), "fsdp", 0)


def chain(state, decay_rows, direction):
    states = state.shape[0]
    packed = jnp.concatenate([state, decay_rows], axis=0).astype(BF)
    total = jnp.zeros_like(state)
    factor = jnp.ones((1, state.shape[1]), F32)
    for step in range(1, lax.axis_size("context")):
        got = shifted(packed, "context", direction * step).astype(F32)
        total = total + factor * got[:states]
        factor = factor * got[states : states + 1]
    return total


def segment_ids(starts, positions):
    counted = jnp.sum((positions[:, None] >= starts[None, 1:]).astype(jnp.int32), axis=1)
    return jnp.where(positions < 0, -1, counted)


def conv_forward(values, edge, weight, shift, segment, edge_segment):
    taps = weight.shape[0]
    length = values.shape[0]
    joined = jnp.concatenate([edge, values], axis=0)
    joined_segment = jnp.concatenate([edge_segment, segment], axis=0)
    summed = jnp.broadcast_to(shift[None, :], values.shape)
    for offset in range(taps):
        matched = joined_segment[offset : offset + length] == segment
        piece = joined[offset : offset + length].astype(F32)
        summed = summed + jnp.where(matched[:, None], piece, 0.0) * weight[offset][None, :]
    return jax.nn.silu(summed).astype(BF)


def body(
    hidden, d_mixed, seq_lengths, norm_gain, w_gate, w_x, w_bc, w_dt, conv_x, conv_x_bias,
    conv_bc, conv_bc_bias, dt_bias, a_log, d_skip, gate_gain, w_out,
):
    row_count, model_width = hidden.shape
    lanes = lax.axis_size("tensor")
    lane = lax.axis_index("tensor")
    share_width = model_width // lanes
    share_start = lane * share_width
    inner_local = conv_x.shape[1]
    inner_width = inner_local * lanes
    heads = dt_bias.shape[0]
    bc_width = conv_bc.shape[1]
    bc_cols = bc_width // lanes
    states = bc_width // 2
    edge_count = conv_x.shape[0] - 1
    lengths = seq_lengths[0]
    count = lengths.shape[0]
    first_row = lax.axis_index("context") * row_count
    starts = (jnp.cumsum(lengths) - lengths).astype(jnp.int32)
    info = jnp.concatenate([first_row.astype(jnp.int32)[None], starts[1:]])
    segment = segment_ids(starts, first_row + jnp.arange(row_count, dtype=jnp.int32))
    edge_segment = segment_ids(
        starts, first_row - edge_count + jnp.arange(edge_count, dtype=jnp.int32)
    )
    spread = (
        lax.broadcasted_iota(jnp.int32, (heads, inner_local), 1) // (inner_local // heads)
        == lax.broadcasted_iota(jnp.int32, (heads, inner_local), 0)
    ).astype(BF)

    x_weight = gather_rows(w_x)
    side_weight = gather_rows(jnp.concatenate([w_bc, w_dt], axis=1))
    gate_weight = gather_rows(w_gate)
    out_weight = gather_rows(w_out.T)

    widened = hidden.astype(F32)
    row_scale = lax.rsqrt(jnp.mean(widened * widened, axis=1, keepdims=True) + EPSILON)
    normed = (widened * row_scale * norm_gain[None, :]).astype(BF)
    x_proj = dot(normed, x_weight).astype(BF)
    side_proj = dot(normed, side_weight).astype(BF)
    bc_proj = side_proj[:, :bc_width]
    dt_proj = side_proj[:, bc_width:]
    z_proj = dot(normed, gate_weight).astype(BF)
    edge = shifted(
        jnp.concatenate(
            [x_proj[row_count - edge_count :], bc_proj[row_count - edge_count :]], axis=1
        ),
        "context",
        1,
    )
    x_edge = edge[:, :inner_local]
    bc_edge = edge[:, inner_local:]
    x_act = conv_forward(x_proj, x_edge, conv_x, conv_x_bias, segment, edge_segment)
    bc_act = conv_forward(bc_proj, bc_edge, conv_bc, conv_bc_bias, segment, edge_segment)
    bias_row, alog_row, skip_row = (dt_bias[None, :], a_log[None, :], d_skip[None, :])
    y_local, full, states_at, final = scan_forward(
        info, count, x_act, bc_act, dt_proj, bias_row, alog_row, spread
    )
    decay_rows = final[states:]
    state_in = chain(final[:states], decay_rows, 1)
    c_rows = bc_act[:, states:]
    full_wide = expand(full, spread)
    y = y_local + dot(c_rows, state_in.astype(BF)) * full_wide
    skip_wide = jnp.repeat(d_skip, inner_local // heads)[None, :]
    y_full = y + skip_wide * x_act.astype(F32)
    z = z_proj.astype(F32)
    sig = jax.nn.sigmoid(z)
    gate = z * sig
    gated = y_full * gate
    squares = total_over(jnp.sum(gated * gated, axis=1), "tensor")
    gate_scale = lax.rsqrt(squares[:, None] / inner_width + EPSILON)
    unit = gated * gate_scale
    normed_out = (unit * gate_gain[None, :]).astype(BF)
    mixed_share = share_over(dot(normed_out, out_weight, NT).astype(BF), "tensor", 1)
    hidden_share = lax.dynamic_slice_in_dim(widened, share_start, share_width, 1)
    mixed = (hidden_share + mixed_share).astype(BF)
    grad_norm_out = dot(d_mixed, out_weight)
    gain_term = jnp.sum(grad_norm_out * unit, axis=0)
    scaled = grad_norm_out * gate_gain[None, :]
    cross = total_over(jnp.sum(scaled * gated, axis=1), "tensor")
    grad_gated = gate_scale * scaled - gated * gate_scale**3 * (cross[:, None] / inner_width)
    dy = (grad_gated * gate).astype(BF)
    grad_zb = (grad_gated * y_full * sig * (1.0 + z * (1.0 - sig))).astype(BF)
    grad_in = dot(c_rows, (dy.astype(F32) * full_wide).astype(BF), TN)
    leaving = chain(grad_in, decay_rows, -1)
    grad_w_out = scatter_rows(dot(d_mixed, normed_out, TN)).T
    grad_w_gate = scatter_rows(dot(normed, grad_zb, TN))
    starting = jnp.concatenate([jnp.ones((1, heads), F32), full[CHUNK - 1 :: CHUNK][:-1]], axis=0)
    starting = jnp.broadcast_to(starting[:, None, :], (starting.shape[0], 8, heads))
    dx_act, dbc_act, ddt, head_sums = scan_backward(
        info, count, x_act, bc_act, dt_proj, bias_row, alog_row, skip_row, spread, y, dy,
        states_at, starting, state_in, leaving,
    )
    dbc_all = total_over(dbc_act.astype(BF), "tensor")
    pad_edge = lambda e: jnp.concatenate([jnp.zeros((8 - edge_count, e.shape[1]), e.dtype), e])
    dx_b, x_tail, x_before, x_grads = conv_back(
        info, count, x_proj, pad_edge(x_edge), dx_act, conv_x, conv_x_bias[None, :]
    )
    dbc_b, bc_tail, bc_before, bc_grads = conv_back(
        info, count, bc_proj, pad_edge(bc_edge), dbc_all, conv_bc, conv_bc_bias[None, :]
    )
    x_next = shifted(x_before, "context", -1)
    bc_next = shifted(bc_before, "context", -1)
    dx_b = lax.dynamic_update_slice(dx_b, (x_tail + x_next).astype(BF), (row_count - 8, 0))
    dbc_b = lax.dynamic_update_slice(dbc_b, (bc_tail + bc_next).astype(BF), (row_count - 8, 0))
    ddt_b = ddt.astype(BF)
    grad_w_x = scatter_rows(dot(normed, dx_b, TN))
    grad_side = scatter_rows(dot(normed, jnp.concatenate([dbc_b, ddt_b], axis=1), TN))
    grad_normed = dot(grad_zb, gate_weight, NT) + dot(dx_b, x_weight, NT)
    dbc_own = lax.dynamic_slice_in_dim(dbc_b, lane * bc_cols, bc_cols, 1)
    bc_weight_own = lax.dynamic_slice_in_dim(side_weight, lane * bc_cols, bc_cols, 1)
    grad_normed = grad_normed + dot(dbc_own, bc_weight_own, NT)
    grad_normed = grad_normed + dot(ddt_b, side_weight[:, bc_width:], NT)
    grad_share = share_over(grad_normed.astype(BF), "tensor", 1)
    gain_share = lax.dynamic_slice_in_dim(norm_gain, share_start, share_width, 0)
    norm_term = jnp.sum(grad_share * hidden_share * row_scale, axis=0)
    gained = grad_share * gain_share[None, :]
    dot_rows = total_over(jnp.sum(gained * hidden_share, axis=1), "tensor")
    dot_rows = dot_rows[:, None] / model_width
    dmix_share = lax.dynamic_slice_in_dim(d_mixed, share_start, share_width, 1)
    grad_hidden = (
        dmix_share.astype(F32) + row_scale * gained - hidden_share * row_scale**3 * dot_rows
    )
    taps = conv_x.shape[0]
    pieces = [
        x_grads[: taps + 1], bc_grads[: taps + 1], head_sums[:3], gain_term, norm_term,
    ]
    flat = jnp.concatenate([p.reshape(-1) for p in pieces])
    padded = -(-flat.shape[0] // 1024) * 1024
    flat = jnp.concatenate([flat, jnp.zeros((padded - flat.shape[0],), F32)]).reshape(-1, 128)
    flat = total_over(total_over(flat, "context"), "fsdp").reshape(-1)
    summed, at = ([], 0)
    for p in pieces:
        size = p.size
        summed.append(flat[at : at + size].reshape(p.shape))
        at += size
    sx, sbc, sh, sgain, snorm = summed
    return (
        mixed, grad_hidden, snorm, grad_w_gate, grad_w_x, grad_side[:, :bc_width],
        grad_side[:, bc_width:], sx[:taps], sx[taps], sbc[:taps], sbc[taps],
        sh[0], sh[1], sh[2], sgain, grad_w_out,
    )


def solution(mesh):
    return jax.shard_map(
        body,
        mesh=mesh,
        in_specs=(
            P(("fsdp", "context"), None),
            P(("fsdp", "context"), None),
            P("fsdp", None),
            P(),
            P(("fsdp", "context"), "tensor"),
            P(("fsdp", "context"), "tensor"),
            P(("fsdp", "context"), None),
            P(("fsdp", "context"), "tensor"),
            P(None, "tensor"),
            P("tensor"),
            P(),
            P(),
            P("tensor"),
            P("tensor"),
            P("tensor"),
            P("tensor"),
            P("tensor", ("fsdp", "context")),
        ),
        out_specs=(
            P(("fsdp", "context"), "tensor"),
            P(("fsdp", "context"), "tensor"),
            P("tensor"),
            P(("fsdp", "context"), "tensor"),
            P(("fsdp", "context"), "tensor"),
            P(("fsdp", "context"), None),
            P(("fsdp", "context"), "tensor"),
            P(None, "tensor"),
            P("tensor"),
            P(),
            P(),
            P("tensor"),
            P("tensor"),
            P("tensor"),
            P("tensor"),
            P("tensor", ("fsdp", "context")),
        ),
        check_vma=False,
    )
```
